32 devices in a mesh: dp: 8 (over z, x), expert: 4 (over y, core).
Axes of the slice: x: 2, y: 2, z: 4, core: 2. Of those that a mesh axis runs over, the one named last changes fastest.
Arguments:
- tokens: bfloat16 [4096, 2048], P(('dp', 'expert')), may hold values from -6 to 6
- d_out: bfloat16 [4096, 2048], P(('dp', 'expert')), may hold values from -6 to 6
- routes: int32 [4096, 2], P(('dp', 'expert')), may hold values from 0 to 3, all different within a row; in each aligned block of 128 rows (0 to 127, 128 to 255, ...) at most 96 rows name the same one
- gate_fixed: int32 [4096, 2], P(('dp', 'expert')), may hold values from 1 to 65535
- w_gate: bfloat16 [4, 2048, 768], P('expert'), may hold values from -0.125 to 0.125
- w_up: bfloat16 [4, 2048, 768], P('expert'), may hold values from -0.125 to 0.125
- w_down: bfloat16 [4, 768, 2048], P('expert'), may hold values from -0.21875 to 0.21875
Outputs:
- d_tokens: bfloat16 [4096, 2048], P(('dp', 'expert'))
- d_wgate: float32 [4, 2048, 768], P('expert', 'dp')
- d_wup: float32 [4, 2048, 768], P('expert', 'dp')
- d_wdown: float32 [4, 768, 2048], P('expert', 'dp')
The draws below stay inside these ranges and needn't reach their ends.
Inputs may be any that keep to these rules, and one draw needn't show every extreme that they name: Each token names 2 different experts; of the routes of one device's 128 tokens (aligned blocks of rows) at most 96 name any one expert, a bound that some block reaches of them.
All inputs are finite; a program needn't handle non-finite values.
Results may differ from the reference program's by a relative error of at most 0.0065.
Values may be sent and summed in bfloat16 or wider, within the bound.
A program may use at most 192 MiB of HBM per device.

```python
import math
import jax
import jax.numpy as jnp
import numpy as np
from jax import lax

D = 2048
I = 768
TOP = 2
TOK_DEV = 128
EXPERTS = 4
CAP = 96
TOKENS = 4096
REPLICAS = 8


def touch_ends(values, stream_key, least, high):
    place = [jax.random.randint(jax.random.fold_in(stream_key, axis), (), 0, length) for axis, length in enumerate(values.shape)]
    widest = values.shape.index(max(values.shape))
    beside = place[:widest] + [(place[widest] + 1) % values.shape[widest]] + place[widest + 1:]
    return values.at[tuple(place)].set(least).at[tuple(beside)].set(high)


def strengthened(values, rng, source, target, parts, factor):
    def block_of(axis_at):
        return (jnp.arange(values.shape[axis_at]) // (values.shape[axis_at] // parts)).reshape((-1,) + (1,) * (values.ndim - 1 - axis_at))

    one_side = jax.random.permutation(rng, parts)[block_of(target)]
    far = (block_of(target) + parts // 2) % parts
    return jnp.where((block_of(source) == one_side) | (block_of(source) == far), factor * values, values)


def block_scale(key, dims, shards, low, top_value):
    def one(position, shards_of):
        steps = jax.random.uniform(jax.random.fold_in(jax.random.fold_in(key, 6), position), (shards_of,), jnp.float32, low / len(shards), top_value / len(shards))
        return jnp.repeat(jnp.exp(steps), dims[position] // shards_of).reshape((-1,) + (1,) * (len(dims) - position - 1))

    gain = one(*shards[0])
    for cut in shards[1:]:
        gain = gain * one(*cut)
    return gain


def routed_block(own_key, own, number, rows, amount, top, most, lean):
    order = jax.random.permutation(own_key, amount)
    packed, common = portions_of(amount, rows * top, most, lean, True), portions_of(amount, rows * top, most, lean, False)
    places = jnp.arange(amount)

    def named(sizes, turn):
        used = int((sizes > 0).sum())
        fixed = max(1, used // 4)
        passed = fixed + (places - fixed + turn * (used - fixed)) % max(1, amount - fixed)
        return jnp.zeros((amount,), jnp.int32).at[order[jnp.where(places < fixed, places, passed)]].set(jnp.asarray(sizes, jnp.int32))

    sizes = jnp.where(number % 4 == 0, named(packed, number // 4), named(common, number - number // 4 - 1))
    mixed = jax.random.permutation(jax.random.fold_in(own, 3), amount)
    giver, receiver = mixed[0:amount // 2 * 2:2], mixed[1:amount // 2 * 2:2]
    margin = jnp.minimum(sizes[giver] - 1, most - sizes[receiver]) // 2
    margin = jnp.where((giver == order[0]) | (receiver == order[0]) | (sizes[receiver] == 0), 0, jnp.maximum(margin, 0))
    passed = jax.random.randint(jax.random.fold_in(own, 4), (amount // 2,), 0, 1 << 20) % (margin + 1)
    sizes = sizes.at[giver].add(-passed).at[receiver].add(passed)
    members = jnp.searchsorted(jnp.cumsum(sizes), jnp.arange(rows * top), side="right").astype(jnp.int32)
    listing = members.reshape(top, rows).T
    listing = listing[jax.random.permutation(jax.random.fold_in(own, 1), rows)]
    turn = jax.random.randint(jax.random.fold_in(own, 2), (rows, 1), 0, top)
    return jnp.take_along_axis(listing, (jnp.arange(top)[None, :] + turn) % top, axis=1)


def portions_of(amount, total, limit, slope, full):
    loads = [(1 << 20) // math.isqrt(standing ** slope) + 1 for standing in range(1, amount + 1)]
    largest = limit if full else min(limit, max(-(-total // amount), total * loads[0] // sum(loads)))
    least = 1 if total - largest >= amount - 1 else 0
    counts, spare = [largest] + [least] * (amount - 1), total - largest - least * (amount - 1)
    while spare > 0:
        candidates = [i for i in range(1, amount) if counts[i] < largest] or [i for i in range(1, amount) if counts[i] < limit]
        pool, budget = sum([loads[i] for i in candidates]), spare
        for i in candidates:
            more = min(limit - counts[i], max(1, budget * loads[i] // pool), spare)
            counts[i] = counts[i] + more
            spare = spare - more
    return np.array(counts)


def scatter_about(rng, dims, width, reach, cuts=(), held_as=jnp.bfloat16):
    entries = jax.random.normal(rng, dims, jnp.float32) * width
    if len(cuts) > 0:
        entries = block_scale(rng, dims, cuts, -0.22, 0.18) * entries
    return jnp.clip(entries, min=-reach, max=reach).astype(held_as)


def bell_draw_with(own_key, shape, deviation, bound, cuts, heavy, kind=jnp.bfloat16):
    entries = deviation * jax.random.normal(own_key, shape, jnp.float32)
    if cuts:
        entries = entries * block_scale(own_key, shape, cuts, -0.22, 0.18)
    return jnp.clip(strengthened(entries, jax.random.fold_in(own_key, 3), *heavy), -bound, bound).astype(kind)


def setup_inputs(seed: int = 0) -> dict:
    key_list = jax.random.split(jax.random.key(seed), 8)
    tokens = bell_draw_with(key_list[0], (TOKENS, D), 1.0, 6.0, ((0, 32),), (0, 1, 32, 2.75))
    d_out = scatter_about(key_list[1], (TOKENS, D), 1.0, 6.0, ((0, 32),))
    routes_keys = jax.random.split(jax.random.fold_in(key_list[2], 1), TOKENS // TOK_DEV)
    routes_turns = jax.random.permutation(jax.random.fold_in(key_list[2], 3), TOKENS // TOK_DEV)
    routes = jax.vmap(lambda own, number: routed_block(jax.random.fold_in(key_list[2], 2), own, number, TOK_DEV, EXPERTS, TOP, CAP, 2))(routes_keys, routes_turns).reshape((TOKENS, TOP))
    gate_fixed = touch_ends(jax.random.randint(key_list[3], (TOKENS, TOP), 1, 65536), jax.random.fold_in(key_list[3], 1), 1, 65535).astype(jnp.int32)
    w_gate = scatter_about(key_list[4], (EXPERTS, D, I), D ** -0.5, 0.125, ((0, 4),))
    w_up = scatter_about(key_list[5], (EXPERTS, D, I), D ** -0.5, 0.125, ((0, 4),))
    w_down = scatter_about(key_list[6], (EXPERTS, I, D), I ** -0.5, 0.21875, ((0, 4),))
    return dict(tokens=tokens, d_out=d_out, routes=routes, gate_fixed=gate_fixed, w_gate=w_gate, w_up=w_up, w_down=w_down)


def reference(tokens, d_out, routes, gate_fixed, w_gate, w_up, w_down):
    token_count, top_count = routes.shape
    route_total = token_count * top_count
    gate_value = (gate_fixed.astype(jnp.float32) / 65536.0).reshape(-1)
    expert_ids = routes.reshape(-1).astype(jnp.int32)
    ordering = jnp.argsort(expert_ids, stable=True).astype(jnp.int32)
    matches = (expert_ids[:, None] == jnp.arange(EXPERTS, dtype=jnp.int32)[None, :]).astype(jnp.int32)
    counting = jnp.sum(matches, axis=0).astype(jnp.int32)
    offsets = (jnp.cumsum(counting) - counting).astype(jnp.int32)
    row_bound = min(CAP * (token_count // TOK_DEV), route_total)
    padded = jnp.concatenate([ordering, jnp.zeros((row_bound,), jnp.int32)])
    inverse = 1.0 / REPLICAS

    def per_expert(accumulated, expert):
        picked = lax.dynamic_slice(padded, (offsets[expert].astype(jnp.int32),), (row_bound,)).astype(jnp.int32)
        live_rows = jnp.arange(row_bound, dtype=jnp.int32) < counting[expert]
        owner_token = (picked // top_count).astype(jnp.int32)
        rows_x = tokens[owner_token]
        scaled = (gate_value[picked][:, None] * d_out[owner_token].astype(jnp.float32)).astype(jnp.bfloat16)
        scaled = jnp.where(live_rows[:, None], scaled, jnp.zeros_like(scaled))
        gate_matrix = w_gate[expert]
        up_matrix = w_up[expert]
        down_matrix = w_down[expert]
        pre_gate = jnp.dot(rows_x, gate_matrix, preferred_element_type=jnp.float32)
        pre_up = jnp.dot(rows_x, up_matrix, preferred_element_type=jnp.float32)
        sigmoid_gate = jax.nn.sigmoid(pre_gate)
        silu_gate = pre_gate * sigmoid_gate
        hidden = (silu_gate * pre_up).astype(jnp.bfloat16)
        d_hidden = jnp.dot(scaled, down_matrix.T, preferred_element_type=jnp.float32)
        d_gate = (d_hidden * pre_up * sigmoid_gate * (1.0 + pre_gate * (1.0 - sigmoid_gate))).astype(jnp.bfloat16)
        d_up = (d_hidden * silu_gate).astype(jnp.bfloat16)
        route_grad = (jnp.dot(d_gate, gate_matrix.T, preferred_element_type=jnp.float32)
                      + jnp.dot(d_up, up_matrix.T, preferred_element_type=jnp.float32)).astype(jnp.bfloat16)
        contribution = jnp.where(live_rows[:, None], route_grad.astype(jnp.float32), jnp.zeros((), jnp.float32))
        accumulated = accumulated.at[owner_token].add(contribution)
        grad_gate = jnp.dot(rows_x.T, d_gate, preferred_element_type=jnp.float32) * inverse
        grad_up = jnp.dot(rows_x.T, d_up, preferred_element_type=jnp.float32) * inverse
        grad_down = jnp.dot(hidden.T, scaled, preferred_element_type=jnp.float32) * inverse
        return accumulated, (grad_gate, grad_up, grad_down)

    start_grad = jnp.zeros((token_count, tokens.shape[1]), jnp.float32)
    accumulated, grads = lax.scan(per_expert, start_grad, jnp.arange(EXPERTS, dtype=jnp.int32))
    return accumulated.astype(jnp.bfloat16), grads[0], grads[1], grads[2]
```

```python
import functools

import jax
import jax.numpy as jnp
from jax import lax
from jax.experimental import pallas as pl
from jax.experimental.pallas import tpu as pltpu
from jax.sharding import PartitionSpec as P

MESH = pl.DeviceIdType.MESH
BF16 = jnp.bfloat16
F32 = jnp.float32


def greet(targets):
    barrier = pltpu.get_barrier_semaphore()
    for target in targets:
        pl.semaphore_signal(barrier, inc=1, device_id=target, device_id_type=MESH)
    pl.semaphore_wait(barrier, len(targets))


def dispatch_kernel(
    span, parts, x_ref, g_ref, c_ref, xs_ref, gs_ref, cs_ref,
    own_sem, core_send, core_recv, chip_send, chip_recv, fwd_send, fwd_recv, c_send, c_recv,
):
    me = lax.axis_index("expert")
    core = lax.rem(me, 2)
    chip = me // 2
    other = chip * 2 + (1 - core)
    chips = span // 2
    greet([{"expert": lax.rem(me + step, span)} for step in range(1, span)])
    rows = x_ref.shape[0] // parts

    def piece(ref, part):
        return ref.at[pl.ds(part * rows, rows)]

    pairs = ((x_ref, xs_ref), (g_ref, gs_ref))
    started, locals_, forwards = [], [], []
    for step in range(1, span):
        copy = pltpu.make_async_remote_copy(
            src_ref=c_ref, dst_ref=cs_ref.at[me], send_sem=c_send.at[step], recv_sem=c_recv.at[step],
            device_id={"expert": lax.rem(me + step, span)}, device_id_type=MESH,
        )
        copy.start()
        started.append(copy)
    chip_copies = []
    for array, (source, target) in enumerate(pairs):
        for part in range(parts):
            for step in range(1, chips):
                there = lax.rem(chip + step, chips) * 2 + core
                copy = pltpu.make_async_remote_copy(
                    src_ref=piece(source, part), dst_ref=piece(target.at[me], part),
                    send_sem=chip_send.at[array, part, step], recv_sem=chip_recv.at[array, part, step],
                    device_id={"expert": there}, device_id_type=MESH,
                )
                copy.start()
                chip_copies.append((array, part, step, copy))
    for array, (source, target) in enumerate(pairs):
        copy = pltpu.make_async_remote_copy(
            src_ref=source, dst_ref=target.at[me], send_sem=core_send.at[array], recv_sem=core_recv.at[array],
            device_id={"expert": other}, device_id_type=MESH,
        )
        copy.start()
        started.append(copy)
        mine = pltpu.make_async_copy(source, target.at[me], own_sem.at[array])
        mine.start()
        locals_.append(mine)
    mine = pltpu.make_async_copy(c_ref, cs_ref.at[me], own_sem.at[2])
    mine.start()
    locals_.append(mine)
    for array, part, step, copy in chip_copies:
        copy.wait_recv()
        owner = lax.rem(chip + chips - step, chips) * 2 + core
        block = piece(pairs[array][1].at[owner], part)
        forward = pltpu.make_async_remote_copy(
            src_ref=block, dst_ref=block,
            send_sem=fwd_send.at[array, part, step], recv_sem=fwd_recv.at[array, part, step],
            device_id={"expert": other}, device_id_type=MESH,
        )
        forward.start()
        forwards.append(forward)
    for copy in locals_:
        copy.wait()
    for _, _, _, copy in chip_copies:
        copy.wait_send()
    for copy in started + forwards:
        copy.wait()


def dispatch(tokens, d_out, coef, span):
    parts = 4
    rows, width = tokens.shape
    lanes = coef.shape[1]
    dma = pltpu.SemaphoreType.DMA
    chips = span // 2
    whole = pl.BlockSpec(memory_space=pltpu.VMEM)
    return pl.pallas_call(
        functools.partial(dispatch_kernel, span, parts),
        out_shape=(
            jax.ShapeDtypeStruct((span, rows, width), BF16),
            jax.ShapeDtypeStruct((span, rows, width), BF16),
            jax.ShapeDtypeStruct((span, rows, lanes), F32),
        ),
        in_specs=[whole] * 3,
        out_specs=[whole] * 3,
        scratch_shapes=[
            dma((3,)), dma((2,)), dma((2,)), dma((2, parts, chips)), dma((2, parts, chips)),
            dma((2, parts, chips)), dma((2, parts, chips)), dma((span,)), dma((span,)),
        ],
        compiler_params=pltpu.CompilerParams(
            collective_id=0, has_side_effects=True, vmem_limit_bytes=40 << 20
        ),
        name="dispatch",
    )(tokens, d_out, coef)


def reduce_kernel(
    span, replicas, gate_ref, up_ref, down_ref, route_ref, gate_out, up_out, down_out, tok_out,
    near_a, near_b, near_c, sum_a, sum_b, sum_c, far_a, far_b, far_c, back,
    near_send, near_recv, far_send, far_recv, back_send, back_recv,
):
    expert = lax.axis_index("expert")
    me = lax.axis_index("dp")
    outer = replicas // 2
    side = lax.rem(me, 2)
    line = me // 2
    grads = (gate_ref, up_ref, down_ref)
    nears = (near_a, near_b, near_c)
    sums = (sum_a, sum_b, sum_c)
    fars = (far_a, far_b, far_c)
    outs = (gate_out, up_out, down_out)
    partner = line * 2 + (1 - side)

    greet(
        [{"expert": lax.rem(expert + step, span)} for step in range(1, span)]
        + [{"dp": partner}]
        + [{"dp": lax.rem(line + step, outer) * 2 + side} for step in range(1, outer)]
    )

    order = [(outer // 2 + k) for k in range(outer - outer // 2)] + list(range(1, outer // 2)) + [0]

    near_copies, far_copies, back_copies = {}, [], []
    for step in order:
        there = lax.rem(line + step, outer)
        for t in range(3):
            copy = pltpu.make_async_remote_copy(
                src_ref=grads[t].at[there * 2 + (1 - side)], dst_ref=nears[t].at[step],
                send_sem=near_send.at[t, step], recv_sem=near_recv.at[t, step],
                device_id={"dp": partner}, device_id_type=MESH,
            )
            copy.start()
            near_copies[t, step] = copy
    for step in range(1, span):
        there = lax.rem(expert + step, span)
        copy = pltpu.make_async_remote_copy(
            src_ref=route_ref.at[there], dst_ref=back.at[step],
            send_sem=back_send.at[step], recv_sem=back_recv.at[step],
            device_id={"expert": there}, device_id_type=MESH,
        )
        copy.start()
        back_copies.append(copy)
    for step in order[:-1]:
        there = lax.rem(line + step, outer)
        for t in range(3):
            near_copies[t, step].wait_recv()
            sums[t][step] = (
                grads[t][there * 2 + side].astype(F32) + nears[t][step].astype(F32)
            ).astype(BF16)
            copy = pltpu.make_async_remote_copy(
                src_ref=sums[t].at[step], dst_ref=fars[t].at[step],
                send_sem=far_send.at[t, step], recv_sem=far_recv.at[t, step],
                device_id={"dp": there * 2 + side}, device_id_type=MESH,
            )
            copy.start()
            far_copies.append(copy)
    for copy in back_copies:
        copy.wait_recv()
    total = route_ref[expert].astype(F32)
    for step in range(1, span):
        total = total + back[step].astype(F32)
    tok_out[...] = total.astype(BF16)
    for t in range(3):
        near_copies[t, 0].wait_recv()
        outs[t][...] = grads[t][line * 2 + side].astype(F32) + nears[t][0].astype(F32)
    at = 0
    for step in order[:-1]:
        for t in range(3):
            far_copies[at].wait_recv()
            at += 1
            outs[t][...] += fars[t][step].astype(F32)
    for copy in list(near_copies.values()) + far_copies + back_copies:
        copy.wait_send()


def reduce_return(grad_gate, grad_up, grad_down, route_grad, span, replicas):
    outer = replicas // 2
    dma = pltpu.SemaphoreType.DMA
    whole = pl.BlockSpec(memory_space=pltpu.VMEM)
    shards = [g.shape[1:] for g in (grad_gate, grad_up, grad_down)]
    slots = [pltpu.VMEM((outer,) + s, BF16) for s in shards]
    rows, width = route_grad.shape[1:]
    return pl.pallas_call(
        functools.partial(reduce_kernel, span, replicas),
        out_shape=tuple(jax.ShapeDtypeStruct(s, F32) for s in shards)
        + (jax.ShapeDtypeStruct((rows, width), BF16),),
        in_specs=[whole] * 4,
        out_specs=[whole] * 4,
        scratch_shapes=slots * 3
        + [pltpu.VMEM((span, rows, width), BF16)]
        + [dma((3, outer)), dma((3, outer)), dma((3, outer)), dma((3, outer)), dma((span,)), dma((span,))],
        compiler_params=pltpu.CompilerParams(
            collective_id=1, has_side_effects=True, vmem_limit_bytes=56 << 20
        ),
        name="reduce_return",
    )(grad_gate, grad_up, grad_down, route_grad)


def body(tokens, d_out, routes, gate_fixed, w_gate, w_up, w_down):
    span = lax.axis_size("expert")
    replicas = lax.axis_size("dp")
    me = lax.axis_index("expert")
    rows, width = tokens.shape
    hidden_units = w_gate.shape[2]
    w_gate, w_up, w_down = w_gate[0], w_up[0], w_down[0]
    lanes = jnp.arange(128, dtype=jnp.int32)
    gate_value = gate_fixed.astype(F32) / 65536.0
    coef = jnp.sum(
        jnp.where(routes[:, :, None] == lanes[None, None, :], gate_value[:, :, None], 0.0), axis=1
    )
    xs, gs, cs = dispatch(tokens, d_out, coef, span)
    x = xs.reshape(span * rows, width)
    weight = jnp.sum(
        jnp.where(lanes[None, :] == me, cs.reshape(span * rows, 128), 0.0), axis=1, keepdims=True
    )
    scaled = (weight * gs.reshape(span * rows, width).astype(F32)).astype(BF16)
    pre_gate = jnp.dot(x, w_gate, preferred_element_type=F32)
    pre_up = jnp.dot(x, w_up, preferred_element_type=F32)
    sigmoid_gate = jax.nn.sigmoid(pre_gate)
    silu_gate = pre_gate * sigmoid_gate
    hidden = (silu_gate * pre_up).astype(BF16)
    d_hidden = lax.dot_general(scaled, w_down, (((1,), (1,)), ((), ())), preferred_element_type=F32)
    d_gate = (d_hidden * pre_up * sigmoid_gate * (1.0 + pre_gate * (1.0 - sigmoid_gate))).astype(BF16)
    d_up = (d_hidden * silu_gate).astype(BF16)
    route_grad = (
        lax.dot_general(d_gate, w_gate, (((1,), (1,)), ((), ())), preferred_element_type=F32)
        + lax.dot_general(d_up, w_up, (((1,), (1,)), ((), ())), preferred_element_type=F32)
    ).astype(BF16)

    def outer_product(left, right):
        return lax.dot_general(
            left, right, (((0,), (0,)), ((), ())), preferred_element_type=F32
        ).astype(BF16)

    grad_gate = outer_product(x, d_gate).reshape(replicas, width // replicas, hidden_units)
    grad_up = outer_product(x, d_up).reshape(replicas, width // replicas, hidden_units)
    grad_down = outer_product(hidden, scaled).reshape(replicas, hidden_units // replicas, width)
    out_gate, out_up, out_down, d_tokens = reduce_return(
        grad_gate, grad_up, grad_down, route_grad.reshape(span, rows, width), span, replicas
    )
    inverse = 1.0 / replicas
    return (d_tokens, (out_gate * inverse)[None], (out_up * inverse)[None], (out_down * inverse)[None])


def solution(mesh):
    rows = P(("dp", "expert"), None)
    whole = P("expert", None, None)
    cut = P("expert", "dp", None)
    return jax.shard_map(
        body, mesh=mesh, in_specs=(rows,) * 4 + (whole,) * 3, out_specs=(rows, cut, cut, cut), check_vma=False
    )
```

```python
import functools

import jax
import jax.numpy as jnp
from jax import lax
from jax.experimental import pallas as pl
from jax.experimental.pallas import tpu as pltpu
from jax.sharding import PartitionSpec as P

MESH = pl.DeviceIdType.MESH
BF16 = jnp.bfloat16
F32 = jnp.float32


def greet(targets):
    barrier = pltpu.get_barrier_semaphore()
    for target in targets:
        pl.semaphore_signal(barrier, inc=1, device_id=target, device_id_type=MESH)
    pl.semaphore_wait(barrier, len(targets))


def dispatch_kernel(
    span, parts, x_ref, g_ref, c_ref, xs_ref, gs_ref, cs_ref,
    own_sem, core_send, core_recv, chip_send, chip_recv, fwd_send, fwd_recv, c_send, c_recv,
):
    me = lax.axis_index("expert")
    core = lax.rem(me, 2)
    chip = me // 2
    other = chip * 2 + (1 - core)
    chips = span // 2
    greet([{"expert": lax.rem(me + step, span)} for step in range(1, span)])
    rows = x_ref.shape[0] // parts

    def piece(ref, part):
        return ref.at[pl.ds(part * rows, rows)]

    pairs = ((x_ref, xs_ref), (g_ref, gs_ref))
    started, locals_, forwards = [], [], []
    for step in range(1, span):
        copy = pltpu.make_async_remote_copy(
            src_ref=c_ref, dst_ref=cs_ref.at[me], send_sem=c_send.at[step], recv_sem=c_recv.at[step],
            device_id={"expert": lax.rem(me + step, span)}, device_id_type=MESH,
        )
        copy.start()
        started.append(copy)
    chip_copies = []
    for array, (source, target) in enumerate(pairs):
        for part in range(parts):
            for step in range(1, chips):
                there = lax.rem(chip + step, chips) * 2 + core
                copy = pltpu.make_async_remote_copy(
                    src_ref=piece(source, part), dst_ref=piece(target.at[me], part),
                    send_sem=chip_send.at[array, part, step], recv_sem=chip_recv.at[array, part, step],
                    device_id={"expert": there}, device_id_type=MESH,
                )
                copy.start()
                chip_copies.append((array, part, step, copy))
    for array, (source, target) in enumerate(pairs):
        copy = pltpu.make_async_remote_copy(
            src_ref=source, dst_ref=target.at[me], send_sem=core_send.at[array], recv_sem=core_recv.at[array],
            device_id={"expert": other}, device_id_type=MESH,
        )
        copy.start()
        started.append(copy)
        mine = pltpu.make_async_copy(source, target.at[me], own_sem.at[array])
        mine.start()
        locals_.append(mine)
    mine = pltpu.make_async_copy(c_ref, cs_ref.at[me], own_sem.at[2])
    mine.start()
    locals_.append(mine)
    for array, part, step, copy in chip_copies:
        copy.wait_recv()
        owner = lax.rem(chip + chips - step, chips) * 2 + core
        block = piece(pairs[array][1].at[owner], part)
        forward = pltpu.make_async_remote_copy(
            src_ref=block, dst_ref=block,
            send_sem=fwd_send.at[array, part, step], recv_sem=fwd_recv.at[array, part, step],
            device_id={"expert": other}, device_id_type=MESH,
        )
        forward.start()
        forwards.append(forward)
    for copy in locals_:
        copy.wait()
    for _, _, _, copy in chip_copies:
        copy.wait_send()
    for copy in started + forwards:
        copy.wait()


def dispatch(tokens, d_out, coef, span):
    parts = 4
    rows, width = tokens.shape
    dma = pltpu.SemaphoreType.DMA
    chips = span // 2
    whole = pl.BlockSpec(memory_space=pltpu.VMEM)
    return pl.pallas_call(
        functools.partial(dispatch_kernel, span, parts),
        out_shape=(
            jax.ShapeDtypeStruct((span, rows, width), BF16),
            jax.ShapeDtypeStruct((span, rows, width), BF16),
            jax.ShapeDtypeStruct((span,) + coef.shape, F32),
        ),
        in_specs=[whole] * 3,
        out_specs=[whole] * 3,
        scratch_shapes=[
            dma((3,)), dma((2,)), dma((2,)), dma((2, parts, chips)), dma((2, parts, chips)),
            dma((2, parts, chips)), dma((2, parts, chips)), dma((span,)), dma((span,)),
        ],
        compiler_params=pltpu.CompilerParams(
            collective_id=0, has_side_effects=True, vmem_limit_bytes=40 << 20
        ),
        name="dispatch",
    )(tokens, d_out, coef)


def reduce_kernel(
    span, replicas, x_ref, scaled_ref, hidden_ref, dg_ref, du_ref, wg_ref, wu_ref,
    gate_out, up_out, down_out, tok_out,
    grad_a, grad_b, grad_c, near_a, near_b, near_c, sum_a, sum_b, sum_c, line_a, line_b, line_c, route, back,
    near_send, near_recv, line_send, line_recv, back_send, back_recv,
):
    expert = lax.axis_index("expert")
    me = lax.axis_index("dp")
    outer = replicas // 2
    side = lax.rem(me, 2)
    line = me // 2
    partner = line * 2 + (1 - side)
    grads = (grad_a, grad_b, grad_c)
    nears = (near_a, near_b, near_c)
    sums = (sum_a, sum_b, sum_c)
    lines = (line_a, line_b, line_c)
    outs = (gate_out, up_out, down_out)
    tensors = (2, 0, 1)
    lower = lax.rem(line + outer - 1, outer) * 2 + side
    upper = lax.rem(line + 1, outer) * 2 + side

    targets = [{"expert": lax.rem(expert + step, span)} for step in range(1, span)]
    targets += [{"dp": partner}, {"dp": lower}, {"dp": upper}]
    greet(targets)

    place = jnp.where(line < outer // 2, 2 * line + 1, 2 * (outer - 1 - line))

    def order_at(i):
        j = i + jnp.where(i >= place, 1, 0)
        half = j // 2
        d = jnp.where(lax.rem(j, 2) == 0, outer - 1 - half, half)
        return jnp.where(i == outer - 1, line, d)

    def near_copy(t, d):
        return pltpu.make_async_remote_copy(
            src_ref=grads[t].at[d * 2 + (1 - side)], dst_ref=nears[t].at[d],
            send_sem=near_send.at[t, d], recv_sem=near_recv.at[t, d],
            device_id={"dp": partner}, device_id_type=MESH,
        )

    def line_copy(t, d):
        following = jnp.where(d > line, line + 1, line - 1)
        slot = jnp.where((d < line) & (d == following), outer, d)
        return pltpu.make_async_remote_copy(
            src_ref=sums[t].at[d], dst_ref=lines[t].at[slot],
            send_sem=line_send.at[t, d], recv_sem=line_recv.at[t, slot],
            device_id={"dp": following * 2 + side}, device_id_type=MESH,
        )

    def line_wait(t, slot):
        pltpu.make_async_remote_copy(
            src_ref=lines[t].at[slot], dst_ref=lines[t].at[slot],
            send_sem=line_send.at[t, 0], recv_sem=line_recv.at[t, slot],
            device_id={"dp": upper}, device_id_type=MESH,
        ).wait_recv()

    def back_copy(step):
        there = lax.rem(expert + step, span)
        return pltpu.make_async_remote_copy(
            src_ref=route.at[step], dst_ref=back.at[step],
            send_sem=back_send.at[step], recv_sem=back_recv.at[step],
            device_id={"expert": there}, device_id_type=MESH,
        )

    def outer_product(left, right):
        return lax.dot_general(left, right, (((0,), (0,)), ((), ())), preferred_element_type=F32)

    units = hidden_ref.shape[1]
    width = units // 2
    shard = units // replicas
    for part in range(2):
        product = outer_product(hidden_ref[:, part * width : (part + 1) * width], scaled_ref[...])
        for piece in range(width // shard):
            grad_c[part * (width // shard) + piece] = product[piece * shard : (piece + 1) * shard].astype(BF16)

    def start_down(i, carry):
        near_copy(2, order_at(i)).start()
        return carry

    lax.fori_loop(0, outer, start_down, 0)
    feature = x_ref.shape[1] // replicas

    def start_pair(i, carry):
        d = order_at(i)
        columns = x_ref[:, pl.ds(pl.multiple_of(d * 2 * feature, 2 * feature), 2 * feature)]
        for t, right in ((0, dg_ref), (1, du_ref)):
            product = outer_product(columns, right[...])
            grads[t][d * 2] = product[:feature].astype(BF16)
            grads[t][d * 2 + 1] = product[feature:].astype(BF16)
            near_copy(t, d).start()
        return carry

    lax.fori_loop(0, outer, start_pair, 0)
    rows = tok_out.shape[0]

    def route_block(step):
        there = lax.rem(expert + step, span)
        at = pl.ds(pl.multiple_of(there * rows, rows), rows)
        contract = (((1,), (1,)), ((), ()))
        route[step] = (
            lax.dot_general(dg_ref[at, :], wg_ref[...], contract, preferred_element_type=F32)
            + lax.dot_general(du_ref[at, :], wu_ref[...], contract, preferred_element_type=F32)
        ).astype(BF16)

    def start_back(step, carry):
        route_block(step)
        back_copy(step).start()
        return carry

    lax.fori_loop(1, span, start_back, 0)

    def forward(i, carry):
        d = order_at(i)
        fed = ((d > line) & (line > 0)) | ((d < line) & (line < outer - 1))
        for t in tensors:
            near_copy(t, d).wait_recv()

            @pl.when(fed)
            def _():
                line_wait(t, d)
                sums[t][d] = (
                    grads[t][d * 2 + side].astype(F32) + nears[t][d].astype(F32) + lines[t][d].astype(F32)
                ).astype(BF16)

            @pl.when(jnp.logical_not(fed))
            def _():
                sums[t][d] = (grads[t][d * 2 + side].astype(F32) + nears[t][d].astype(F32)).astype(BF16)

            line_copy(t, d).start()
        return carry

    lax.fori_loop(0, outer - 1, forward, 0)
    route_block(0)
    for step in range(1, span):
        back_copy(step).wait_recv()
    total = route[0].astype(F32)
    for step in range(1, span):
        total = total + back[step].astype(F32)
    tok_out[...] = total.astype(BF16)
    for t in tensors:
        near_copy(t, line).wait_recv()
        outs[t][...] = grads[t][me].astype(F32) + nears[t][line].astype(F32)

        @pl.when(line > 0)
        def _():
            line_wait(t, line)
            outs[t][...] += lines[t][line].astype(F32)

        @pl.when(line < outer - 1)
        def _():
            line_wait(t, outer)
            outs[t][...] += lines[t][outer].astype(F32)

    def finish(i, carry):
        d = order_at(i)
        for t in range(3):
            near_copy(t, d).wait_send()

            @pl.when(i < outer - 1)
            def _():
                line_copy(t, d).wait_send()

        return carry

    lax.fori_loop(0, outer, finish, 0)
    for step in range(1, span):
        back_copy(step).wait_send()


def reduce_return(x, scaled, hidden, d_gate, d_up, w_gate, w_up, span, replicas):
    outer = replicas // 2
    dma = pltpu.SemaphoreType.DMA
    whole = pl.BlockSpec(memory_space=pltpu.VMEM)
    width, units = x.shape[1], hidden.shape[1]
    rows = x.shape[0] // span
    shards = [(width // replicas, units)] * 2 + [(units // replicas, width)]
    return pl.pallas_call(
        functools.partial(reduce_kernel, span, replicas),
        out_shape=tuple(jax.ShapeDtypeStruct(s, F32) for s in shards)
        + (jax.ShapeDtypeStruct((rows, width), BF16),),
        in_specs=[whole] * 7,
        out_specs=[whole] * 4,
        scratch_shapes=[pltpu.VMEM((replicas,) + s, BF16) for s in shards]
        + [pltpu.VMEM((outer,) + s, BF16) for s in shards] * 2
        + [pltpu.VMEM((outer + 1,) + s, BF16) for s in shards]
        + [pltpu.VMEM((span, rows, width), BF16)] * 2
        + [dma((3, outer)), dma((3, outer)), dma((3, outer)), dma((3, outer + 1)), dma((span,)), dma((span,))],
        compiler_params=pltpu.CompilerParams(
            collective_id=1, has_side_effects=True, vmem_limit_bytes=60 << 20
        ),
        name="reduce_return",
    )(x, scaled, hidden, d_gate, d_up, w_gate, w_up)


def body(tokens, d_out, routes, gate_fixed, w_gate, w_up, w_down):
    span = lax.axis_size("expert")
    replicas = lax.axis_size("dp")
    me = lax.axis_index("expert")
    rows, width = tokens.shape
    hidden_units = w_gate.shape[2]
    w_gate, w_up, w_down = w_gate[0], w_up[0], w_down[0]
    places = jnp.arange(max(8, span), dtype=jnp.int32)
    gate_value = gate_fixed.astype(F32) / 65536.0
    coef = jnp.sum(
        jnp.where(places[:, None, None] == routes[None], gate_value[None], 0.0), axis=2
    )
    xs, gs, cs = dispatch(tokens, d_out, coef, span)
    x = xs.reshape(span * rows, width)
    weight = jnp.sum(jnp.where(places[None, :, None] == me, cs, 0.0), axis=1).reshape(span * rows, 1)
    scaled = (weight * gs.reshape(span * rows, width).astype(F32)).astype(BF16)
    pre_gate = jnp.dot(x, w_gate, preferred_element_type=F32)
    pre_up = jnp.dot(x, w_up, preferred_element_type=F32)
    sigmoid_gate = jax.nn.sigmoid(pre_gate)
    silu_gate = pre_gate * sigmoid_gate
    hidden = (silu_gate * pre_up).astype(BF16)
    d_hidden = lax.dot_general(scaled, w_down, (((1,), (1,)), ((), ())), preferred_element_type=F32)
    d_gate = (d_hidden * pre_up * sigmoid_gate * (1.0 + pre_gate * (1.0 - sigmoid_gate))).astype(BF16)
    d_up = (d_hidden * silu_gate).astype(BF16)
    out_gate, out_up, out_down, d_tokens = reduce_return(
        x, scaled, hidden, d_gate, d_up, w_gate, w_up, span, replicas
    )
    inverse = 1.0 / replicas
    return (d_tokens, (out_gate * inverse)[None], (out_up * inverse)[None], (out_down * inverse)[None])


def solution(mesh):
    rows = P(("dp", "expert"), None)
    whole = P("expert", None, None)
    cut = P("expert", "dp", None)
    return jax.shard_map(
        body, mesh=mesh, in_specs=(rows,) * 4 + (whole,) * 3, out_specs=(rows, cut, cut, cut), check_vma=False
    )
```

```python
import functools

import jax
import jax.numpy as jnp
from jax import lax
from jax.experimental import pallas as pl
from jax.experimental.pallas import tpu as pltpu
from jax.sharding import PartitionSpec as P

MESH = pl.DeviceIdType.MESH
BF16 = jnp.bfloat16
F32 = jnp.float32


def greet(targets):
    barrier = pltpu.get_barrier_semaphore()
    for target in targets:
        pl.semaphore_signal(barrier, inc=1, device_id=target, device_id_type=MESH)
    pl.semaphore_wait(barrier, len(targets))


def dispatch_kernel(
    span, parts, x_ref, g_ref, c_ref, xs_ref, gs_ref, cs_ref,
    own_sem, core_send, core_recv, chip_send, chip_recv, fwd_send, fwd_recv, c_send, c_recv,
):
    me = lax.axis_index("expert")
    core = lax.rem(me, 2)
    chip = me // 2
    other = chip * 2 + (1 - core)
    chips = span // 2
    greet([{"expert": lax.rem(me + step, span)} for step in range(1, span)])
    rows = x_ref.shape[0] // parts

    def piece(ref, part):
        return ref.at[pl.ds(part * rows, rows)]

    pairs = ((x_ref, xs_ref), (g_ref, gs_ref))
    started, locals_, forwards = [], [], []
    for step in range(1, span):
        copy = pltpu.make_async_remote_copy(
            src_ref=c_ref, dst_ref=cs_ref.at[me], send_sem=c_send.at[step], recv_sem=c_recv.at[step],
            device_id={"expert": lax.rem(me + step, span)}, device_id_type=MESH,
        )
        copy.start()
        started.append(copy)
    chip_copies = []
    for array, (source, target) in enumerate(pairs):
        for part in range(parts):
            for step in range(1, chips):
                there = lax.rem(chip + step, chips) * 2 + core
                copy = pltpu.make_async_remote_copy(
                    src_ref=piece(source, part), dst_ref=piece(target.at[me], part),
                    send_sem=chip_send.at[array, part, step], recv_sem=chip_recv.at[array, part, step],
                    device_id={"expert": there}, device_id_type=MESH,
                )
                copy.start()
                chip_copies.append((array, part, step, copy))
    for array, (source, target) in enumerate(pairs):
        copy = pltpu.make_async_remote_copy(
            src_ref=source, dst_ref=target.at[me], send_sem=core_send.at[array], recv_sem=core_recv.at[array],
            device_id={"expert": other}, device_id_type=MESH,
        )
        copy.start()
        started.append(copy)
        mine = pltpu.make_async_copy(source, target.at[me], own_sem.at[array])
        mine.start()
        locals_.append(mine)
    mine = pltpu.make_async_copy(c_ref, cs_ref.at[me], own_sem.at[2])
    mine.start()
    locals_.append(mine)
    for array, part, step, copy in chip_copies:
        copy.wait_recv()
        owner = lax.rem(chip + chips - step, chips) * 2 + core
        block = piece(pairs[array][1].at[owner], part)
        forward = pltpu.make_async_remote_copy(
            src_ref=block, dst_ref=block,
            send_sem=fwd_send.at[array, part, step], recv_sem=fwd_recv.at[array, part, step],
            device_id={"expert": other}, device_id_type=MESH,
        )
        forward.start()
        forwards.append(forward)
    for copy in locals_:
        copy.wait()
    for _, _, _, copy in chip_copies:
        copy.wait_send()
    for copy in started + forwards:
        copy.wait()


def dispatch(tokens, d_out, coef, span):
    parts = 4
    rows, width = tokens.shape
    dma = pltpu.SemaphoreType.DMA
    chips = span // 2
    whole = pl.BlockSpec(memory_space=pltpu.VMEM)
    return pl.pallas_call(
        functools.partial(dispatch_kernel, span, parts),
        out_shape=(
            jax.ShapeDtypeStruct((span, rows, width), BF16),
            jax.ShapeDtypeStruct((span, rows, width), BF16),
            jax.ShapeDtypeStruct((span,) + coef.shape, F32),
        ),
        in_specs=[whole] * 3,
        out_specs=[whole] * 3,
        scratch_shapes=[
            dma((3,)), dma((2,)), dma((2,)), dma((2, parts, chips)), dma((2, parts, chips)),
            dma((2, parts, chips)), dma((2, parts, chips)), dma((span,)), dma((span,)),
        ],
        compiler_params=pltpu.CompilerParams(
            collective_id=0, has_side_effects=True, vmem_limit_bytes=40 << 20
        ),
        name="dispatch",
    )(tokens, d_out, coef)


def reduce_kernel(
    span, replicas, x_ref, scaled_ref, hidden_ref, dg_ref, du_ref, wg_ref, wu_ref,
    gate_out, up_out, down_out, tok_out,
    grad_a, grad_b, grad_c, near_a, near_b, near_c, sum_a, sum_b, sum_c, line_a, line_b, line_c, route, back,
    grad_z, sum_z, line_z, total_z, cross_out, cross_in,
    near_send, near_recv, line_send, line_recv, back_send, back_recv, cross_send, cross_recv,
):
    expert = lax.axis_index("expert")
    me = lax.axis_index("dp")
    outer = replicas // 2
    side = lax.rem(me, 2)
    line = me // 2
    partner = line * 2 + (1 - side)
    grads = (grad_a, grad_b, grad_c)
    nears = (near_a, near_b, near_c)
    sums = (sum_a, sum_b, sum_c, sum_z)
    lines = (line_a, line_b, line_c, line_z)
    half = down_out.shape[1] // 2
    outs = (gate_out, up_out, down_out.at[:, half:])
    tensors = (2, 0, 1)
    lower = lax.rem(line + outer - 1, outer) * 2 + side
    upper = lax.rem(line + 1, outer) * 2 + side

    targets = [{"expert": lax.rem(expert + step, span)} for step in range(1, span)]
    targets += [{"dp": partner}, {"dp": lower}, {"dp": upper}]
    greet(targets)

    place = jnp.where(line < outer // 2, 2 * line + 1, 2 * (outer - 1 - line))

    def order_at(i):
        j = i + jnp.where(i >= place, 1, 0)
        d = jnp.where(lax.rem(j, 2) == 0, outer - 1 - j // 2, j // 2)
        return jnp.where(i == outer - 1, line, d)

    def near_copy(t, d):
        return pltpu.make_async_remote_copy(
            src_ref=grads[t].at[d * 2 + (1 - side)], dst_ref=nears[t].at[d],
            send_sem=near_send.at[t, d], recv_sem=near_recv.at[t, d],
            device_id={"dp": partner}, device_id_type=MESH,
        )

    def line_copy(t, d, source=None):
        following = jnp.where(d > line, line + 1, line - 1)
        slot = jnp.where((d < line) & (d == following), outer, d)
        return pltpu.make_async_remote_copy(
            src_ref=sums[t].at[d] if source is None else source, dst_ref=lines[t].at[slot],
            send_sem=line_send.at[t, d], recv_sem=line_recv.at[t, slot],
            device_id={"dp": following * 2 + side}, device_id_type=MESH,
        )

    def line_wait(t, slot):
        pltpu.make_async_remote_copy(
            src_ref=lines[t].at[slot], dst_ref=lines[t].at[slot],
            send_sem=line_send.at[t, 0], recv_sem=line_recv.at[t, slot],
            device_id={"dp": upper}, device_id_type=MESH,
        ).wait_recv()

    def back_copy(step):
        there = lax.rem(expert + step, span)
        return pltpu.make_async_remote_copy(
            src_ref=route.at[step], dst_ref=back.at[step],
            send_sem=back_send.at[step], recv_sem=back_recv.at[step],
            device_id={"expert": there}, device_id_type=MESH,
        )

    def outer_product(left, right):
        return lax.dot_general(left, right, (((0,), (0,)), ((), ())), preferred_element_type=F32)

    def is_fed(d):
        return ((d > line) & (line > 0)) | ((d < line) & (line < outer - 1))

    cross = pltpu.make_async_remote_copy(
        src_ref=cross_out, dst_ref=cross_in, send_sem=cross_send, recv_sem=cross_recv,
        device_id={"dp": partner}, device_id_type=MESH,
    )
    units = hidden_ref.shape[1]
    width = units // 2
    shard = units // replicas

    def down_product(target, columns):
        for part in range(2):
            product = outer_product(hidden_ref[:, part * width : (part + 1) * width], scaled_ref[:, columns])
            for piece in range(width // shard):
                target[part * (width // shard) + piece] = product[piece * shard : (piece + 1) * shard].astype(BF16)

    def both(d):
        return grad_z.at[pl.ds(d * 2, 2)]

    down_product(grad_z, slice(0, half))

    def start_line(i, carry):
        d = order_at(i)

        @pl.when(jnp.logical_not(is_fed(d)))
        def _():
            line_copy(3, d, both(d)).start()

        return carry

    lax.fori_loop(0, outer - 1, start_line, 0)
    down_product(grad_c, slice(half, 2 * half))
    near_copy(2, order_at(0)).start()
    feature = x_ref.shape[1] // replicas

    def make_pair(i, carry):
        d = order_at(i)
        columns = x_ref[:, pl.ds(pl.multiple_of(d * 2 * feature, 2 * feature), 2 * feature)]
        for t, right in ((0, dg_ref), (1, du_ref)):
            product = outer_product(columns, right[...])
            grads[t][d * 2] = product[:feature].astype(BF16)
            grads[t][d * 2 + 1] = product[feature:].astype(BF16)

            @pl.when(i == 0)
            def _():
                near_copy(t, d).start()

        return carry

    lax.fori_loop(0, outer, make_pair, 0)

    def feed_line(i, carry):
        d = order_at(i)

        @pl.when(is_fed(d))
        def _():
            line_wait(3, d)
            sum_z[d] = (grad_z[pl.ds(d * 2, 2)].astype(F32) + line_z[d].astype(F32)).astype(BF16)
            line_copy(3, d).start()

        return carry

    lax.fori_loop(0, outer - 1, feed_line, 0)
    rows = tok_out.shape[0]

    def route_block(step):
        there = lax.rem(expert + step, span)
        at = pl.ds(pl.multiple_of(there * rows, rows), rows)
        contract = (((1,), (1,)), ((), ()))
        route[step] = (
            lax.dot_general(dg_ref[at, :], wg_ref[...], contract, preferred_element_type=F32)
            + lax.dot_general(du_ref[at, :], wu_ref[...], contract, preferred_element_type=F32)
        ).astype(BF16)

    def start_back(step, carry):
        route_block(step)
        back_copy(step).start()
        return carry

    lax.fori_loop(1, span, start_back, 0)

    def forward(i, carry):
        d = order_at(i)
        fed = is_fed(d)

        @pl.when(i == max(outer // 2 - 1, 0))
        def _():
            total_z[...] = grad_z[pl.ds(line * 2, 2)].astype(F32)

            @pl.when(line > 0)
            def _():
                line_wait(3, line)
                total_z[...] += line_z[line].astype(F32)

            @pl.when(line < outer - 1)
            def _():
                line_wait(3, outer)
                total_z[...] += line_z[outer].astype(F32)

            cross_out[...] = total_z[1 - side].astype(BF16)
            cross.start()

        for t in tensors:
            near_copy(t, d).wait_recv()
            near_copy(t, order_at(i + 1)).start()

            @pl.when(fed)
            def _():
                line_wait(t, d)
                sums[t][d] = (
                    grads[t][d * 2 + side].astype(F32) + nears[t][d].astype(F32) + lines[t][d].astype(F32)
                ).astype(BF16)

            @pl.when(jnp.logical_not(fed))
            def _():
                sums[t][d] = (grads[t][d * 2 + side].astype(F32) + nears[t][d].astype(F32)).astype(BF16)

            line_copy(t, d).start()
        return carry

    lax.fori_loop(0, outer - 1, forward, 0)
    route_block(0)
    for step in range(1, span):
        back_copy(step).wait_recv()
    total = route[0].astype(F32)
    for step in range(1, span):
        total = total + back[step].astype(F32)
    tok_out[...] = total.astype(BF16)
    cross.wait_recv()
    down_out[:, :half] = total_z[side] + cross_in[...].astype(F32)
    for t in tensors:
        near_copy(t, line).wait_recv()
        outs[t][...] = grads[t][me].astype(F32) + nears[t][line].astype(F32)

        @pl.when(line > 0)
        def _():
            line_wait(t, line)
            outs[t][...] += lines[t][line].astype(F32)

        @pl.when(line < outer - 1)
        def _():
            line_wait(t, outer)
            outs[t][...] += lines[t][outer].astype(F32)

    def finish(i, carry):
        d = order_at(i)
        for t in range(3):
            near_copy(t, d).wait_send()

        @pl.when(i < outer - 1)
        def _():
            for t in range(4):
                line_copy(t, d).wait_send()

        return carry

    lax.fori_loop(0, outer, finish, 0)
    cross.wait_send()
    for step in range(1, span):
        back_copy(step).wait_send()


def reduce_return(x, scaled, hidden, d_gate, d_up, w_gate, w_up, span, replicas):
    outer = replicas // 2
    dma = pltpu.SemaphoreType.DMA
    whole = pl.BlockSpec(memory_space=pltpu.VMEM)
    width, units = x.shape[1], hidden.shape[1]
    rows = x.shape[0] // span
    shards = [(width // replicas, units)] * 2 + [(units // replicas, width)]
    parts = shards[:2] + [(units // replicas, width // 2)]
    return pl.pallas_call(
        functools.partial(reduce_kernel, span, replicas),
        out_shape=tuple(jax.ShapeDtypeStruct(s, F32) for s in shards)
        + (jax.ShapeDtypeStruct((rows, width), BF16),),
        in_specs=[whole] * 7,
        out_specs=[whole] * 4,
        scratch_shapes=[pltpu.VMEM((replicas,) + s, BF16) for s in parts]
        + [pltpu.VMEM((outer,) + s, BF16) for s in parts] * 2
        + [pltpu.VMEM((outer + 1,) + s, BF16) for s in parts]
        + [pltpu.VMEM((span, rows, width), BF16)] * 2
        + [
            pltpu.VMEM((replicas,) + parts[2], BF16),
            pltpu.VMEM((outer, 2) + parts[2], BF16),
            pltpu.VMEM((outer + 1, 2) + parts[2], BF16),
            pltpu.VMEM((2,) + parts[2], F32),
            pltpu.VMEM(parts[2], BF16),
            pltpu.VMEM(parts[2], BF16),
        ]
        + [dma((3, outer)), dma((3, outer)), dma((4, outer)), dma((4, outer + 1)), dma((span,)), dma((span,)), dma, dma],
        compiler_params=pltpu.CompilerParams(
            collective_id=1, has_side_effects=True, vmem_limit_bytes=60 << 20
        ),
        name="reduce_return",
    )(x, scaled, hidden, d_gate, d_up, w_gate, w_up)


def body(tokens, d_out, routes, gate_fixed, w_gate, w_up, w_down):
    span = lax.axis_size("expert")
    replicas = lax.axis_size("dp")
    me = lax.axis_index("expert")
    rows, width = tokens.shape
    hidden_units = w_gate.shape[2]
    w_gate, w_up, w_down = w_gate[0], w_up[0], w_down[0]
    places = jnp.arange(max(8, span), dtype=jnp.int32)
    gate_value = gate_fixed.astype(F32) / 65536.0
    coef = jnp.sum(
        jnp.where(places[:, None, None] == routes[None], gate_value[None], 0.0), axis=2
    )
    xs, gs, cs = dispatch(tokens, d_out, coef, span)
    x = xs.reshape(span * rows, width)
    weight = jnp.sum(jnp.where(places[None, :, None] == me, cs, 0.0), axis=1).reshape(span * rows, 1)
    scaled = (weight * gs.reshape(span * rows, width).astype(F32)).astype(BF16)
    pre_gate = jnp.dot(x, w_gate, preferred_element_type=F32)
    pre_up = jnp.dot(x, w_up, preferred_element_type=F32)
    sigmoid_gate = jax.nn.sigmoid(pre_gate)
    silu_gate = pre_gate * sigmoid_gate
    hidden = (silu_gate * pre_up).astype(BF16)
    d_hidden = lax.dot_general(scaled, w_down, (((1,), (1,)), ((), ())), preferred_element_type=F32)
    d_gate = (d_hidden * pre_up * sigmoid_gate * (1.0 + pre_gate * (1.0 - sigmoid_gate))).astype(BF16)
    d_up = (d_hidden * silu_gate).astype(BF16)
    out_gate, out_up, out_down, d_tokens = reduce_return(
        x, scaled, hidden, d_gate, d_up, w_gate, w_up, span, replicas
    )
    inverse = 1.0 / replicas
    return (d_tokens, (out_gate * inverse)[None], (out_up * inverse)[None], (out_down * inverse)[None])


def solution(mesh):
    rows = P(("dp", "expert"), None)
    whole = P("expert", None, None)
    cut = P("expert", "dp", None)
    return jax.shard_map(
        body, mesh=mesh, in_specs=(rows,) * 4 + (whole,) * 3, out_specs=(rows, cut, cut, cut), check_vma=False
    )
```

```python
import functools

import jax
import jax.numpy as jnp
from jax import lax
from jax.experimental import pallas as pl
from jax.experimental.pallas import tpu as pltpu
from jax.sharding import PartitionSpec as P

MESH = pl.DeviceIdType.MESH
BF16 = jnp.bfloat16
F32 = jnp.float32


def greet(targets):
    barrier = pltpu.get_barrier_semaphore()
    for target in targets:
        pl.semaphore_signal(barrier, inc=1, device_id=target, device_id_type=MESH)
    pl.semaphore_wait(barrier, len(targets))


def dispatch_kernel(
    span, parts, x_ref, g_ref, c_ref, xs_ref, gs_ref, cs_ref,
    own_sem, core_send, core_recv, chip_send, chip_recv, fwd_send, fwd_recv, c_send, c_recv,
):
    me = lax.axis_index("expert")
    core = lax.rem(me, 2)
    chip = me // 2
    other = chip * 2 + (1 - core)
    chips = span // 2
    greet([{"expert": lax.rem(me + step, span)} for step in range(1, span)])
    rows = x_ref.shape[0] // parts

    def piece(ref, part):
        return ref.at[pl.ds(part * rows, rows)]

    pairs = ((x_ref, xs_ref), (g_ref, gs_ref))
    started, locals_, forwards = [], [], []
    for step in range(1, span):
        copy = pltpu.make_async_remote_copy(
            src_ref=c_ref, dst_ref=cs_ref.at[me], send_sem=c_send.at[step], recv_sem=c_recv.at[step],
            device_id={"expert": lax.rem(me + step, span)}, device_id_type=MESH,
        )
        copy.start()
        started.append(copy)
    chip_copies = []
    for array, (source, target) in enumerate(pairs):
        for part in range(parts):
            for step in range(1, chips):
                there = lax.rem(chip + step, chips) * 2 + core
                copy = pltpu.make_async_remote_copy(
                    src_ref=piece(source, part), dst_ref=piece(target.at[me], part),
                    send_sem=chip_send.at[array, part, step], recv_sem=chip_recv.at[array, part, step],
                    device_id={"expert": there}, device_id_type=MESH,
                )
                copy.start()
                chip_copies.append((array, part, step, copy))
    for array, (source, target) in enumerate(pairs):
        copy = pltpu.make_async_remote_copy(
            src_ref=source, dst_ref=target.at[me], send_sem=core_send.at[array], recv_sem=core_recv.at[array],
            device_id={"expert": other}, device_id_type=MESH,
        )
        copy.start()
        started.append(copy)
        mine = pltpu.make_async_copy(source, target.at[me], own_sem.at[array])
        mine.start()
        locals_.append(mine)
    mine = pltpu.make_async_copy(c_ref, cs_ref.at[me], own_sem.at[2])
    mine.start()
    locals_.append(mine)
    for array, part, step, copy in chip_copies:
        copy.wait_recv()
        owner = lax.rem(chip + chips - step, chips) * 2 + core
        block = piece(pairs[array][1].at[owner], part)
        forward = pltpu.make_async_remote_copy(
            src_ref=block, dst_ref=block,
            send_sem=fwd_send.at[array, part, step], recv_sem=fwd_recv.at[array, part, step],
            device_id={"expert": other}, device_id_type=MESH,
        )
        forward.start()
        forwards.append(forward)
    for copy in locals_:
        copy.wait()
    for _, _, _, copy in chip_copies:
        copy.wait_send()
    for copy in started + forwards:
        copy.wait()


def dispatch(tokens, d_out, coef, span):
    parts = 4
    rows, width = tokens.shape
    dma = pltpu.SemaphoreType.DMA
    chips = span // 2
    whole = pl.BlockSpec(memory_space=pltpu.VMEM)
    return pl.pallas_call(
        functools.partial(dispatch_kernel, span, parts),
        out_shape=(
            jax.ShapeDtypeStruct((span, rows, width), BF16),
            jax.ShapeDtypeStruct((span, rows, width), BF16),
            jax.ShapeDtypeStruct((span,) + coef.shape, F32),
        ),
        in_specs=[whole] * 3,
        out_specs=[whole] * 3,
        scratch_shapes=[
            dma((3,)), dma((2,)), dma((2,)), dma((2, parts, chips)), dma((2, parts, chips)),
            dma((2, parts, chips)), dma((2, parts, chips)), dma((span,)), dma((span,)),
        ],
        compiler_params=pltpu.CompilerParams(
            collective_id=0, has_side_effects=True, vmem_limit_bytes=40 << 20
        ),
        name="dispatch",
    )(tokens, d_out, coef)


def reduce_kernel(
    span, replicas, x_ref, scaled_ref, hidden_ref, dg_ref, du_ref, wg_ref, wu_ref,
    gate_out, up_out, down_out, tok_out,
    grad_a, grad_b, grad_c, near_a, near_b, near_c, sum_a, sum_b, sum_c, line_a, line_b, line_c, route, back,
    grad_z, sum_z, line_z, total_z, cross_out, cross_in,
    near_send, near_recv, line_send, line_recv, back_send, back_recv, cross_send, cross_recv,
):
    expert = lax.axis_index("expert")
    me = lax.axis_index("dp")
    outer = replicas // 2
    side = lax.rem(me, 2)
    line = me // 2
    partner = line * 2 + (1 - side)
    grads = (grad_a, grad_b, grad_c)
    nears = (near_a, near_b, near_c)
    sums = (sum_a, sum_b, sum_c, sum_z)
    lines = (line_a, line_b, line_c, line_z)
    half = down_out.shape[1] // 2
    outs = (gate_out, up_out, down_out.at[:, half:])
    tensors = (2, 0, 1)
    lower = lax.rem(line + outer - 1, outer) * 2 + side
    upper = lax.rem(line + 1, outer) * 2 + side

    targets = [{"expert": lax.rem(expert + step, span)} for step in range(1, span)]
    targets += [{"dp": partner}, {"dp": lower}, {"dp": upper}]
    greet(targets)

    place = jnp.where(line < outer // 2, 2 * line + 1, 2 * (outer - 1 - line))

    def order_at(i):
        j = i + jnp.where(i >= place, 1, 0)
        d = jnp.where(lax.rem(j, 2) == 0, outer - 1 - j // 2, j // 2)
        return jnp.where(i == outer - 1, line, d)

    def near_copy(t, d):
        return pltpu.make_async_remote_copy(
            src_ref=grads[t].at[d * 2 + (1 - side)], dst_ref=nears[t].at[d],
            send_sem=near_send.at[t, d], recv_sem=near_recv.at[t, d],
            device_id={"dp": partner}, device_id_type=MESH,
        )

    def line_copy(t, d, source=None):
        following = jnp.where(d > line, line + 1, line - 1)
        slot = jnp.where((d < line) & (d == following), outer, d)
        return pltpu.make_async_remote_copy(
            src_ref=sums[t].at[d] if source is None else source, dst_ref=lines[t].at[slot],
            send_sem=line_send.at[t, d], recv_sem=line_recv.at[t, slot],
            device_id={"dp": following * 2 + side}, device_id_type=MESH,
        )

    def line_wait(t, slot):
        pltpu.make_async_remote_copy(
            src_ref=lines[t].at[slot], dst_ref=lines[t].at[slot],
            send_sem=line_send.at[t, 0], recv_sem=line_recv.at[t, slot],
            device_id={"dp": upper}, device_id_type=MESH,
        ).wait_recv()

    def back_copy(step):
        there = lax.rem(expert + step, span)
        return pltpu.make_async_remote_copy(
            src_ref=route.at[step], dst_ref=back.at[step],
            send_sem=back_send.at[step], recv_sem=back_recv.at[step],
            device_id={"expert": there}, device_id_type=MESH,
        )

    def outer_product(left, right):
        return lax.dot_general(left, right, (((0,), (0,)), ((), ())), preferred_element_type=F32)

    def is_fed(d):
        return ((d > line) & (line > 0)) | ((d < line) & (line < outer - 1))

    cross = pltpu.make_async_remote_copy(
        src_ref=cross_out, dst_ref=cross_in, send_sem=cross_send, recv_sem=cross_recv,
        device_id={"dp": partner}, device_id_type=MESH,
    )
    units = hidden_ref.shape[1]
    width = units // 2
    shard = units // replicas

    def down_product(target, columns):
        for part in range(2):
            product = outer_product(hidden_ref[:, part * width : (part + 1) * width], scaled_ref[:, columns])
            for piece in range(width // shard):
                target[part * (width // shard) + piece] = product[piece * shard : (piece + 1) * shard].astype(BF16)

    def both(d):
        return grad_z.at[pl.ds(d * 2, 2)]

    down_product(grad_z, slice(0, half))

    def start_line(i, carry):
        d = order_at(i)

        @pl.when(jnp.logical_not(is_fed(d)))
        def _():
            line_copy(3, d, both(d)).start()

        return carry

    lax.fori_loop(0, outer - 1, start_line, 0)
    down_product(grad_c, slice(half, 2 * half))
    near_copy(2, order_at(0)).start()
    feature = x_ref.shape[1] // replicas

    def make_pair(i, carry):
        d = order_at(i)
        columns = x_ref[:, pl.ds(pl.multiple_of(d * 2 * feature, 2 * feature), 2 * feature)]
        for t, right in ((0, dg_ref), (1, du_ref)):
            product = outer_product(columns, right[...])
            grads[t][d * 2] = product[:feature].astype(BF16)
            grads[t][d * 2 + 1] = product[feature:].astype(BF16)

            @pl.when(i == 0)
            def _():
                near_copy(t, d).start()

        return carry

    lax.fori_loop(0, outer, make_pair, 0)

    def feed_line(i, carry):
        d = order_at(i)

        @pl.when(is_fed(d))
        def _():
            line_wait(3, d)
            sum_z[d] = (grad_z[pl.ds(d * 2, 2)].astype(F32) + line_z[d].astype(F32)).astype(BF16)
            line_copy(3, d).start()

        return carry

    lax.fori_loop(0, outer - 1, feed_line, 0)
    rows = tok_out.shape[0]

    def route_block(step):
        there = lax.rem(expert + step, span)
        at = pl.ds(pl.multiple_of(there * rows, rows), rows)
        contract = (((1,), (1,)), ((), ()))
        route[step] = (
            lax.dot_general(dg_ref[at, :], wg_ref[...], contract, preferred_element_type=F32)
            + lax.dot_general(du_ref[at, :], wu_ref[...], contract, preferred_element_type=F32)
        ).astype(BF16)

    def start_back(step, carry):
        route_block(step)
        back_copy(step).start()
        return carry

    lax.fori_loop(1, span, start_back, 0)

    def forward(i, carry):
        d = order_at(i)
        fed = is_fed(d)

        @pl.when(i == max(outer // 2 - 1, 0))
        def _():
            total_z[...] = grad_z[pl.ds(line * 2, 2)].astype(F32)

            @pl.when(line > 0)
            def _():
                line_wait(3, line)
                total_z[...] += line_z[line].astype(F32)

            @pl.when(line < outer - 1)
            def _():
                line_wait(3, outer)
                total_z[...] += line_z[outer].astype(F32)

            cross_out[...] = total_z[1 - side].astype(BF16)
            cross.start()

        for k, t in enumerate(tensors):
            near_copy(t, d).wait_recv()
            near_copy(t, order_at(i + 1)).start()

            @pl.when(fed)
            def _():
                line_wait(t, d)
                sums[t][d] = (
                    grads[t][d * 2 + side].astype(F32) + nears[t][d].astype(F32) + lines[t][d].astype(F32)
                ).astype(BF16)

            @pl.when(jnp.logical_not(fed))
            def _():
                sums[t][d] = (grads[t][d * 2 + side].astype(F32) + nears[t][d].astype(F32)).astype(BF16)

            if k == 0:

                @pl.when(i > 0)
                def _():
                    line_copy(tensors[2], order_at(i - 1)).wait_send()

            else:
                line_copy(tensors[k - 1], d).wait_send()
            line_copy(t, d).start()
        return carry

    lax.fori_loop(0, outer - 1, forward, 0)
    route_block(0)
    for step in range(1, span):
        back_copy(step).wait_recv()
    total = route[0].astype(F32)
    for step in range(1, span):
        total = total + back[step].astype(F32)
    tok_out[...] = total.astype(BF16)
    cross.wait_recv()
    down_out[:, :half] = total_z[side] + cross_in[...].astype(F32)
    for t in tensors:
        near_copy(t, line).wait_recv()
        outs[t][...] = grads[t][me].astype(F32) + nears[t][line].astype(F32)

        @pl.when(line > 0)
        def _():
            line_wait(t, line)
            outs[t][...] += lines[t][line].astype(F32)

        @pl.when(line < outer - 1)
        def _():
            line_wait(t, outer)
            outs[t][...] += lines[t][outer].astype(F32)

    def finish(i, carry):
        d = order_at(i)
        for t in range(3):
            near_copy(t, d).wait_send()

        @pl.when(i < outer - 1)
        def _():
            line_copy(3, d).wait_send()

        return carry

    lax.fori_loop(0, outer, finish, 0)
    if outer > 1:
        line_copy(tensors[2], order_at(outer - 2)).wait_send()
    cross.wait_send()
    for step in range(1, span):
        back_copy(step).wait_send()


def reduce_return(x, scaled, hidden, d_gate, d_up, w_gate, w_up, span, replicas):
    outer = replicas // 2
    dma = pltpu.SemaphoreType.DMA
    whole = pl.BlockSpec(memory_space=pltpu.VMEM)
    width, units = x.shape[1], hidden.shape[1]
    rows = x.shape[0] // span
    shards = [(width // replicas, units)] * 2 + [(units // replicas, width)]
    parts = shards[:2] + [(units // replicas, width // 2)]
    return pl.pallas_call(
        functools.partial(reduce_kernel, span, replicas),
        out_shape=tuple(jax.ShapeDtypeStruct(s, F32) for s in shards)
        + (jax.ShapeDtypeStruct((rows, width), BF16),),
        in_specs=[whole] * 7,
        out_specs=[whole] * 4,
        scratch_shapes=[pltpu.VMEM((replicas,) + s, BF16) for s in parts]
        + [pltpu.VMEM((outer,) + s, BF16) for s in parts] * 2
        + [pltpu.VMEM((outer + 1,) + s, BF16) for s in parts]
        + [pltpu.VMEM((span, rows, width), BF16)] * 2
        + [
            pltpu.VMEM((replicas,) + parts[2], BF16),
            pltpu.VMEM((outer, 2) + parts[2], BF16),
            pltpu.VMEM((outer + 1, 2) + parts[2], BF16),
            pltpu.VMEM((2,) + parts[2], F32),
            pltpu.VMEM(parts[2], BF16),
            pltpu.VMEM(parts[2], BF16),
        ]
        + [dma((3, outer)), dma((3, outer)), dma((4, outer)), dma((4, outer + 1)), dma((span,)), dma((span,)), dma, dma],
        compiler_params=pltpu.CompilerParams(
            collective_id=1, has_side_effects=True, vmem_limit_bytes=60 << 20
        ),
        name="reduce_return",
    )(x, scaled, hidden, d_gate, d_up, w_gate, w_up)


def body(tokens, d_out, routes, gate_fixed, w_gate, w_up, w_down):
    span = lax.axis_size("expert")
    replicas = lax.axis_size("dp")
    me = lax.axis_index("expert")
    rows, width = tokens.shape
    hidden_units = w_gate.shape[2]
    w_gate, w_up, w_down = w_gate[0], w_up[0], w_down[0]
    places = jnp.arange(max(8, span), dtype=jnp.int32)
    gate_value = gate_fixed.astype(F32) / 65536.0
    coef = jnp.sum(
        jnp.where(places[:, None, None] == routes[None], gate_value[None], 0.0), axis=2
    )
    xs, gs, cs = dispatch(tokens, d_out, coef, span)
    x = xs.reshape(span * rows, width)
    weight = jnp.sum(jnp.where(places[None, :, None] == me, cs, 0.0), axis=1).reshape(span * rows, 1)
    scaled = (weight * gs.reshape(span * rows, width).astype(F32)).astype(BF16)
    pre_gate = jnp.dot(x, w_gate, preferred_element_type=F32)
    pre_up = jnp.dot(x, w_up, preferred_element_type=F32)
    sigmoid_gate = jax.nn.sigmoid(pre_gate)
    silu_gate = pre_gate * sigmoid_gate
    hidden = (silu_gate * pre_up).astype(BF16)
    d_hidden = lax.dot_general(scaled, w_down, (((1,), (1,)), ((), ())), preferred_element_type=F32)
    d_gate = (d_hidden * pre_up * sigmoid_gate * (1.0 + pre_gate * (1.0 - sigmoid_gate))).astype(BF16)
    d_up = (d_hidden * silu_gate).astype(BF16)
    out_gate, out_up, out_down, d_tokens = reduce_return(
        x, scaled, hidden, d_gate, d_up, w_gate, w_up, span, replicas
    )
    inverse = 1.0 / replicas
    return (d_tokens, (out_gate * inverse)[None], (out_up * inverse)[None], (out_down * inverse)[None])


def solution(mesh):
    rows = P(("dp", "expert"), None)
    whole = P("expert", None, None)
    cut = P("expert", "dp", None)
    return jax.shard_map(
        body, mesh=mesh, in_specs=(rows,) * 4 + (whole,) * 3, out_specs=(rows, cut, cut, cut), check_vma=False
    )
```

```python
import functools

import jax
import jax.numpy as jnp
from jax import lax
from jax.experimental import pallas as pl
from jax.experimental.pallas import tpu as pltpu
from jax.sharding import PartitionSpec as P

MESH = pl.DeviceIdType.MESH
BF16 = jnp.bfloat16
F32 = jnp.float32


def greet(targets):
    barrier = pltpu.get_barrier_semaphore()
    for target in targets:
        pl.semaphore_signal(barrier, inc=1, device_id=target, device_id_type=MESH)
    pl.semaphore_wait(barrier, len(targets))


def dispatch_kernel(
    span, parts, x_ref, g_ref, c_ref, wg_ref, wu_ref, xs_ref, gs_ref, cs_ref, gate_ref, up_ref,
    own_sem, core_send, core_recv, chip_send, chip_recv, fwd_send, fwd_recv, c_send, c_recv,
):
    me = lax.axis_index("expert")
    core = lax.rem(me, 2)
    chip = me // 2
    other = chip * 2 + (1 - core)
    chips = span // 2
    greet([{"expert": lax.rem(me + step, span)} for step in range(1, span)])
    rows = x_ref.shape[0] // parts

    def piece(ref, part):
        return ref.at[pl.ds(part * rows, rows)]

    pairs = ((x_ref, xs_ref), (g_ref, gs_ref))
    started, locals_, forwards = [], [], []
    for step in range(1, span):
        copy = pltpu.make_async_remote_copy(
            src_ref=c_ref, dst_ref=cs_ref.at[me], send_sem=c_send.at[step], recv_sem=c_recv.at[step],
            device_id={"expert": lax.rem(me + step, span)}, device_id_type=MESH,
        )
        copy.start()
        started.append(copy)
    chip_copies = []
    for array, (source, target) in enumerate(pairs):
        for part in range(parts):
            for step in range(1, chips):
                there = lax.rem(chip + step, chips) * 2 + core
                copy = pltpu.make_async_remote_copy(
                    src_ref=piece(source, part), dst_ref=piece(target.at[me], part),
                    send_sem=chip_send.at[array, part, step], recv_sem=chip_recv.at[array, part, step],
                    device_id={"expert": there}, device_id_type=MESH,
                )
                copy.start()
                chip_copies.append((array, part, step, copy))
    for array, (source, target) in enumerate(pairs):
        copy = pltpu.make_async_remote_copy(
            src_ref=source, dst_ref=target.at[me], send_sem=core_send.at[array], recv_sem=core_recv.at[array],
            device_id={"expert": other}, device_id_type=MESH,
        )
        copy.start()
        started.append(copy)
        mine = pltpu.make_async_copy(source, target.at[me], own_sem.at[array])
        mine.start()
        locals_.append(mine)
    mine = pltpu.make_async_copy(c_ref, cs_ref.at[me], own_sem.at[2])
    mine.start()
    locals_.append(mine)

    def project(owner, block):
        gate_ref[owner] = jnp.dot(block[...], wg_ref[...], preferred_element_type=F32)
        up_ref[owner] = jnp.dot(block[...], wu_ref[...], preferred_element_type=F32)

    project(me, x_ref)
    started[span - 1].wait_recv()
    project(other, xs_ref.at[other])
    passed = {}
    for array in range(2):
        for number, part, step, copy in chip_copies:
            if number == array:
                copy.wait_recv()
                owner = lax.rem(chip + chips - step, chips) * 2 + core
                block = piece(pairs[array][1].at[owner], part)
                forward = pltpu.make_async_remote_copy(
                    src_ref=block, dst_ref=block,
                    send_sem=fwd_send.at[array, part, step], recv_sem=fwd_recv.at[array, part, step],
                    device_id={"expert": other}, device_id_type=MESH,
                )
                forward.start()
                passed[array, part, step] = forward
        if array == 0:
            for step in range(1, chips):
                there = lax.rem(chip + chips - step, chips) * 2
                project(there + core, xs_ref.at[there + core])
                for part in range(parts):
                    owner = there + (1 - core)
                    block = piece(xs_ref.at[owner], part)
                    pltpu.make_async_remote_copy(
                        src_ref=block, dst_ref=block,
                        send_sem=fwd_send.at[0, part, step], recv_sem=fwd_recv.at[0, part, step],
                        device_id={"expert": other}, device_id_type=MESH,
                    ).wait_recv()
                project(there + (1 - core), xs_ref.at[there + (1 - core)])
    for copy in locals_:
        copy.wait()
    for _, _, _, copy in chip_copies:
        copy.wait_send()
    for at, copy in enumerate(started):
        copy.wait_send()
        if at != span - 1:
            copy.wait_recv()
    for (array, _, _), forward in passed.items():
        forward.wait_send()
        if array == 1:
            forward.wait_recv()


def dispatch(tokens, d_out, coef, w_gate, w_up, span):
    parts = 4
    rows, width = tokens.shape
    dma = pltpu.SemaphoreType.DMA
    chips = span // 2
    whole = pl.BlockSpec(memory_space=pltpu.VMEM)
    return pl.pallas_call(
        functools.partial(dispatch_kernel, span, parts),
        out_shape=(
            jax.ShapeDtypeStruct((span, rows, width), BF16),
            jax.ShapeDtypeStruct((span, rows, width), BF16),
            jax.ShapeDtypeStruct((span,) + coef.shape, F32),
            jax.ShapeDtypeStruct((span, rows, w_gate.shape[1]), F32),
            jax.ShapeDtypeStruct((span, rows, w_gate.shape[1]), F32),
        ),
        in_specs=[whole] * 5,
        out_specs=[whole] * 5,
        scratch_shapes=[
            dma((3,)), dma((2,)), dma((2,)), dma((2, parts, chips)), dma((2, parts, chips)),
            dma((2, parts, chips)), dma((2, parts, chips)), dma((span,)), dma((span,)),
        ],
        compiler_params=pltpu.CompilerParams(
            collective_id=0, has_side_effects=True, vmem_limit_bytes=40 << 20
        ),
        name="dispatch",
    )(tokens, d_out, coef, w_gate, w_up)


def reduce_kernel(
    span, replicas, x_ref, scaled_ref, hidden_ref, dg_ref, du_ref, wg_ref, wu_ref,
    gate_out, up_out, down_out, tok_out,
    grad_a, grad_b, grad_c, near_a, near_b, near_c, sum_a, sum_b, sum_c, line_a, line_b, line_c, route, back,
    grad_z, sum_z, line_z, total_z, cross_out, cross_in,
    near_send, near_recv, line_send, line_recv, back_send, back_recv, cross_send, cross_recv,
):
    expert = lax.axis_index("expert")
    me = lax.axis_index("dp")
    outer = replicas // 2
    side = lax.rem(me, 2)
    line = me // 2
    partner = line * 2 + (1 - side)
    grads = (grad_a, grad_b, grad_c)
    nears = (near_a, near_b, near_c)
    sums = (sum_a, sum_b, sum_c, sum_z)
    lines = (line_a, line_b, line_c, line_z)
    cut = down_out.shape[1] // 4
    outs = (gate_out, up_out, down_out.at[:, cut:])
    tensors = (2, 0, 1)
    lower = lax.rem(line + outer - 1, outer) * 2 + side
    upper = lax.rem(line + 1, outer) * 2 + side

    targets = [{"expert": lax.rem(expert + step, span)} for step in range(1, span)]
    targets += [{"dp": partner}, {"dp": lower}, {"dp": upper}]
    greet(targets)

    place = jnp.where(line < outer // 2, 2 * line + 1, 2 * (outer - 1 - line))

    def order_at(i):
        j = i + jnp.where(i >= place, 1, 0)
        d = jnp.where(lax.rem(j, 2) == 0, outer - 1 - j // 2, j // 2)
        return jnp.where(i == outer - 1, line, d)

    def near_copy(t, d):
        return pltpu.make_async_remote_copy(
            src_ref=grads[t].at[d * 2 + (1 - side)], dst_ref=nears[t].at[d],
            send_sem=near_send.at[t, d], recv_sem=near_recv.at[t, d],
            device_id={"dp": partner}, device_id_type=MESH,
        )

    def line_copy(t, d, source=None):
        following = jnp.where(d > line, line + 1, line - 1)
        slot = jnp.where((d < line) & (d == following), outer, d)
        return pltpu.make_async_remote_copy(
            src_ref=sums[t].at[d] if source is None else source, dst_ref=lines[t].at[slot],
            send_sem=line_send.at[t, d], recv_sem=line_recv.at[t, slot],
            device_id={"dp": following * 2 + side}, device_id_type=MESH,
        )

    def line_wait(t, slot):
        pltpu.make_async_remote_copy(
            src_ref=lines[t].at[slot], dst_ref=lines[t].at[slot],
            send_sem=line_send.at[t, 0], recv_sem=line_recv.at[t, slot],
            device_id={"dp": upper}, device_id_type=MESH,
        ).wait_recv()

    def back_copy(step):
        there = lax.rem(expert + step, span)
        return pltpu.make_async_remote_copy(
            src_ref=route.at[step], dst_ref=back.at[step],
            send_sem=back_send.at[step], recv_sem=back_recv.at[step],
            device_id={"expert": there}, device_id_type=MESH,
        )

    def outer_product(left, right):
        return lax.dot_general(left, right, (((0,), (0,)), ((), ())), preferred_element_type=F32)

    def is_fed(d):
        return ((d > line) & (line > 0)) | ((d < line) & (line < outer - 1))

    cross = pltpu.make_async_remote_copy(
        src_ref=cross_out, dst_ref=cross_in, send_sem=cross_send, recv_sem=cross_recv,
        device_id={"dp": partner}, device_id_type=MESH,
    )
    units = hidden_ref.shape[1]
    width = units // 2
    shard = units // replicas

    def down_product(target, columns):
        for part in range(2):
            product = outer_product(hidden_ref[:, part * width : (part + 1) * width], scaled_ref[:, columns])
            for piece in range(width // shard):
                target[part * (width // shard) + piece] = product[piece * shard : (piece + 1) * shard].astype(BF16)

    def both(d):
        return grad_z.at[pl.ds(d * 2, 2)]

    down_product(grad_z, slice(0, cut))

    def start_line(i, carry):
        d = order_at(i)

        @pl.when(jnp.logical_not(is_fed(d)))
        def _():
            line_copy(3, d, both(d)).start()

        return carry

    lax.fori_loop(0, outer - 1, start_line, 0)
    down_product(grad_c, slice(cut, down_out.shape[1]))
    near_copy(2, order_at(0)).start()
    feature = x_ref.shape[1] // replicas

    def make_pair(i, carry):
        d = order_at(i)
        columns = x_ref[:, pl.ds(pl.multiple_of(d * 2 * feature, 2 * feature), 2 * feature)]
        for t, right in ((0, dg_ref), (1, du_ref)):
            product = outer_product(columns, right[...])
            grads[t][d * 2] = product[:feature].astype(BF16)
            grads[t][d * 2 + 1] = product[feature:].astype(BF16)

            @pl.when(i == 0)
            def _():
                near_copy(t, d).start()

        return carry

    lax.fori_loop(0, outer, make_pair, 0)

    def feed_line(i, carry):
        d = order_at(i)

        @pl.when(is_fed(d))
        def _():
            line_wait(3, d)
            sum_z[d] = (grad_z[pl.ds(d * 2, 2)].astype(F32) + line_z[d].astype(F32)).astype(BF16)
            line_copy(3, d).start()

        return carry

    lax.fori_loop(0, outer - 1, feed_line, 0)
    rows = tok_out.shape[0]

    def route_block(step):
        there = lax.rem(expert + step, span)
        at = pl.ds(pl.multiple_of(there * rows, rows), rows)
        contract = (((1,), (1,)), ((), ()))
        route[step] = (
            lax.dot_general(dg_ref[at, :], wg_ref[...], contract, preferred_element_type=F32)
            + lax.dot_general(du_ref[at, :], wu_ref[...], contract, preferred_element_type=F32)
        ).astype(BF16)

    def start_back(step, carry):
        route_block(step)
        back_copy(step).start()
        return carry

    lax.fori_loop(1, span, start_back, 0)

    def forward(i, carry):
        d = order_at(i)
        fed = is_fed(d)

        @pl.when(i == max(outer // 2 - 1, 0))
        def _():
            total_z[...] = grad_z[pl.ds(line * 2, 2)].astype(F32)

            @pl.when(line > 0)
            def _():
                line_wait(3, line)
                total_z[...] += line_z[line].astype(F32)

            @pl.when(line < outer - 1)
            def _():
                line_wait(3, outer)
                total_z[...] += line_z[outer].astype(F32)

            cross_out[...] = total_z[1 - side].astype(BF16)
            cross.start()

        for t in tensors:
            near_copy(t, d).wait_recv()
            near_copy(t, order_at(i + 1)).start()

            @pl.when(fed)
            def _():
                line_wait(t, d)
                sums[t][d] = (
                    grads[t][d * 2 + side].astype(F32) + nears[t][d].astype(F32) + lines[t][d].astype(F32)
                ).astype(BF16)

            @pl.when(jnp.logical_not(fed))
            def _():
                sums[t][d] = (grads[t][d * 2 + side].astype(F32) + nears[t][d].astype(F32)).astype(BF16)

            line_copy(t, d).start()
        return carry

    lax.fori_loop(0, outer - 1, forward, 0)
    route_block(0)
    for step in range(1, span):
        back_copy(step).wait_recv()
    total = route[0].astype(F32)
    for step in range(1, span):
        total = total + back[step].astype(F32)
    tok_out[...] = total.astype(BF16)
    cross.wait_recv()
    down_out[:, :cut] = total_z[side] + cross_in[...].astype(F32)
    for t in tensors:
        near_copy(t, line).wait_recv()
        outs[t][...] = grads[t][me].astype(F32) + nears[t][line].astype(F32)

        @pl.when(line > 0)
        def _():
            line_wait(t, line)
            outs[t][...] += lines[t][line].astype(F32)

        @pl.when(line < outer - 1)
        def _():
            line_wait(t, outer)
            outs[t][...] += lines[t][outer].astype(F32)

    def finish(i, carry):
        d = order_at(i)
        for t in range(3):
            near_copy(t, d).wait_send()

        @pl.when(i < outer - 1)
        def _():
            for t in range(4):
                line_copy(t, d).wait_send()

        return carry

    lax.fori_loop(0, outer, finish, 0)
    cross.wait_send()
    for step in range(1, span):
        back_copy(step).wait_send()


def reduce_return(x, scaled, hidden, d_gate, d_up, w_gate, w_up, span, replicas):
    outer = replicas // 2
    dma = pltpu.SemaphoreType.DMA
    whole = pl.BlockSpec(memory_space=pltpu.VMEM)
    width, units = x.shape[1], hidden.shape[1]
    rows = x.shape[0] // span
    shards = [(width // replicas, units)] * 2 + [(units // replicas, width)]
    parts = shards[:2] + [(units // replicas, width - width // 4)]
    early = (units // replicas, width // 4)
    return pl.pallas_call(
        functools.partial(reduce_kernel, span, replicas),
        out_shape=tuple(jax.ShapeDtypeStruct(s, F32) for s in shards)
        + (jax.ShapeDtypeStruct((rows, width), BF16),),
        in_specs=[whole] * 7,
        out_specs=[whole] * 4,
        scratch_shapes=[pltpu.VMEM((replicas,) + s, BF16) for s in parts]
        + [pltpu.VMEM((outer,) + s, BF16) for s in parts] * 2
        + [pltpu.VMEM((outer + 1,) + s, BF16) for s in parts]
        + [pltpu.VMEM((span, rows, width), BF16)] * 2
        + [
            pltpu.VMEM((replicas,) + early, BF16),
            pltpu.VMEM((outer, 2) + early, BF16),
            pltpu.VMEM((outer + 1, 2) + early, BF16),
            pltpu.VMEM((2,) + early, F32),
            pltpu.VMEM(early, BF16),
            pltpu.VMEM(early, BF16),
        ]
        + [dma((3, outer)), dma((3, outer)), dma((4, outer)), dma((4, outer + 1)), dma((span,)), dma((span,)), dma, dma],
        compiler_params=pltpu.CompilerParams(
            collective_id=1, has_side_effects=True, vmem_limit_bytes=60 << 20
        ),
        name="reduce_return",
    )(x, scaled, hidden, d_gate, d_up, w_gate, w_up)


def body(tokens, d_out, routes, gate_fixed, w_gate, w_up, w_down):
    span = lax.axis_size("expert")
    replicas = lax.axis_size("dp")
    me = lax.axis_index("expert")
    rows, width = tokens.shape
    hidden_units = w_gate.shape[2]
    w_gate, w_up, w_down = w_gate[0], w_up[0], w_down[0]
    places = jnp.arange(max(8, span), dtype=jnp.int32)
    gate_value = gate_fixed.astype(F32) / 65536.0
    coef = jnp.sum(
        jnp.where(places[:, None, None] == routes[None], gate_value[None], 0.0), axis=2
    )
    xs, gs, cs, pre_gate, pre_up = dispatch(tokens, d_out, coef, w_gate, w_up, span)
    x = xs.reshape(span * rows, width)
    weight = jnp.sum(jnp.where(places[None, :, None] == me, cs, 0.0), axis=1).reshape(span * rows, 1)
    scaled = (weight * gs.reshape(span * rows, width).astype(F32)).astype(BF16)
    pre_gate = pre_gate.reshape(span * rows, hidden_units)
    pre_up = pre_up.reshape(span * rows, hidden_units)
    sigmoid_gate = jax.nn.sigmoid(pre_gate)
    silu_gate = pre_gate * sigmoid_gate
    hidden = (silu_gate * pre_up).astype(BF16)
    d_hidden = lax.dot_general(scaled, w_down, (((1,), (1,)), ((), ())), preferred_element_type=F32)
    d_gate = (d_hidden * pre_up * sigmoid_gate * (1.0 + pre_gate * (1.0 - sigmoid_gate))).astype(BF16)
    d_up = (d_hidden * silu_gate).astype(BF16)
    out_gate, out_up, out_down, d_tokens = reduce_return(
        x, scaled, hidden, d_gate, d_up, w_gate, w_up, span, replicas
    )
    inverse = 1.0 / replicas
    return (d_tokens, (out_gate * inverse)[None], (out_up * inverse)[None], (out_down * inverse)[None])


def solution(mesh):
    rows = P(("dp", "expert"), None)
    whole = P("expert", None, None)
    cut = P("expert", "dp", None)
    return jax.shard_map(
        body, mesh=mesh, in_specs=(rows,) * 4 + (whole,) * 3, out_specs=(rows, cut, cut, cut), check_vma=False
    )
```
